32 devices in a mesh: fsdp: 8 (over z, core), ctx: 2 (over x), tp: 2 (over y).
Axes of the slice: x: 2, y: 2, z: 4, core: 2. Of those that a mesh axis runs over, the one named last changes fastest.
Arguments:
- block_input: bfloat16 [8, 384, 1024], P('fsdp', 'ctx'), may hold values from -6 to 6
- segments: int32 [8, 384], P('fsdp', 'ctx'), may hold values from 0 to 3, never falling along the last dimension, each value on 1 to 192 neighbouring positions
- norm1_gain: bfloat16 [1024], P('fsdp'), may hold values from 0.5 to 1.5
- q_weight: bfloat16 [1024, 1024], P('fsdp', 'tp'), may hold values from -0.1875 to 0.1875
- k_weight: bfloat16 [1024, 1024], P('fsdp', 'tp'), may hold values from -0.1875 to 0.1875
- v_weight: bfloat16 [1024, 2048], P('fsdp', 'tp'), may hold values from -0.1875 to 0.1875
- decay_weight: bfloat16 [1024, 8], P('fsdp', 'tp'), may hold values from -0.1875 to 0.1875
- beta_weight: bfloat16 [1024, 8], P('fsdp', 'tp'), may hold values from -0.1875 to 0.1875
- gate_weight: bfloat16 [1024, 2048], P('fsdp', 'tp'), may hold values from -0.1875 to 0.1875
- conv_weight: bfloat16 [4096, 4], P(('tp', 'fsdp')), may hold values from -3 to 3
- decay_rate: float32 [8], P('tp'), may hold values from 0.0005 to 0.05
- head_gain: bfloat16 [256], P('fsdp'), may hold values from 0.5 to 1.5
- out_weight: bfloat16 [1024, 2048], P('fsdp', 'tp'), may hold values from -0.25 to 0.25
- norm2_gain: bfloat16 [1024], P('fsdp'), may hold values from 0.5 to 1.5
- ffn_gate: bfloat16 [1024, 2816], P('fsdp', 'tp'), may hold values from -0.1875 to 0.1875
- ffn_up: bfloat16 [1024, 2816], P('fsdp', 'tp'), may hold values from -0.1875 to 0.1875
- ffn_down: bfloat16 [1024, 2816], P('fsdp', 'tp'), may hold values from -0.109375 to 0.109375
- cotangent: bfloat16 [8, 384, 1024], P('fsdp', 'ctx'), may hold values from -6 to 6
Outputs:
- block_output: bfloat16 [8, 384, 1024], P('fsdp', 'ctx')
- input_grad: float32 [8, 384, 1024], P('fsdp', 'ctx')
- norm1_gain_grad: float32 [1024], P('fsdp')
- q_weight_grad: float32 [1024, 1024], P('fsdp', 'tp')
- k_weight_grad: float32 [1024, 1024], P('fsdp', 'tp')
- v_weight_grad: float32 [1024, 2048], P('fsdp', 'tp')
- decay_weight_grad: float32 [1024, 8], P('fsdp', 'tp')
- beta_weight_grad: float32 [1024, 8], P('fsdp', 'tp')
- gate_weight_grad: float32 [1024, 2048], P('fsdp', 'tp')
- conv_weight_grad: float32 [4096, 4], P(('tp', 'fsdp'))
- decay_rate_grad: float32 [8], P('tp')
- head_gain_grad: float32 [256], P('fsdp')
- out_weight_grad: float32 [1024, 2048], P('fsdp', 'tp')
- norm2_gain_grad: float32 [1024], P('fsdp')
- ffn_gate_grad: float32 [1024, 2816], P('fsdp', 'tp')
- ffn_up_grad: float32 [1024, 2816], P('fsdp', 'tp')
- ffn_down_grad: float32 [1024, 2816], P('fsdp', 'tp')
The draws below stay inside these ranges and needn't reach their ends.
Inputs may be any that keep to these rules, and one draw needn't show every extreme that they name: `segments`: segment numbers never fall along a sequence; a document has 1 to 192 tokens and one document of each sequence has exactly 192.
All inputs are finite; a program needn't handle non-finite values.
Results may differ from the reference program's by a relative error of at most 0.014.
Values may be sent and summed in bfloat16 or wider, within the bound.
A program may use at most 192 MiB of HBM per device.

```python
import math
import jax
import jax.numpy as jnp
import numpy as np
from jax import lax

D = 1024
H = 8
DK = 128
DV = 256
FF = 2816
CONV = 4
GROUP = 64
LEN = 384
SEQS = 8


def block_levels(key, shape, pieces, least, high):
    gain = 1.0
    for dim, shards_of in pieces:
        steps = jax.random.uniform(jax.random.fold_in(jax.random.fold_in(key, 6), dim), (shards_of,), jnp.float32, least / len(pieces), high / len(pieces))
        gain = gain * jnp.repeat(jnp.exp(steps), shape[dim] // shards_of).reshape((-1,) + (1,) * (len(shape) - 1 - dim))
    return gain


def length_profile(count, total, most, lean):
    loads = [(1 << 20) // math.isqrt(grade ** lean) + 1 for grade in range(2, count + 1)]
    spare, given = total - most - (count - 1), [1] * (count - 1)
    while spare > 0:
        movable = [i for i in range(count - 1) if given[i] < most]
        whole, left = sum([loads[i] for i in movable]), spare
        for i in movable:
            addition = min(most - given[i], max(1, left * loads[i] // whole), spare)
            given[i] = given[i] + addition
            spare = spare - addition
    return np.array([most] + given)


def ragged(key, amount, total, bound, lean):
    if amount == 2:
        one = jax.random.randint(key, (), max(1, total - bound), min(bound, total - 1) + 1)
        return jnp.stack([one, total - one])
    lengths = jnp.asarray(length_profile(amount, total, bound, lean), jnp.int32)
    pairs = (amount - 1) // 2
    donor, sink = lengths[1:1 + 2 * pairs:2], lengths[2:2 + 2 * pairs:2]
    room = jnp.minimum(donor - 1, bound - sink)
    shifted = jax.random.randint(jax.random.fold_in(key, 1), (pairs,), 0, 1 << 20) % (room + 1)
    lengths = lengths.at[1:1 + 2 * pairs:2].set(donor - shifted).at[2:2 + 2 * pairs:2].set(sink + shifted)
    return lengths[jax.random.permutation(jax.random.fold_in(key, 2), amount)]


def bell_draw(rng, dims, deviation, bound, pieces=(), kind=jnp.bfloat16):
    entries = jax.random.normal(rng, dims, jnp.float32) * deviation
    if len(pieces) > 0:
        entries = block_levels(rng, dims, pieces, -0.22, 0.18) * entries
    return jnp.clip(entries, min=-bound, max=bound).astype(kind)


def setup_inputs(seed: int = 0) -> dict:
    seeds = jax.random.split(jax.random.key(seed), 19)
    return {
        "block_input": bell_draw(seeds[0], (SEQS, LEN, D), 1.0, 6.0, ((0, 8), (1, 2))),
        "segments": jax.vmap(lambda own: jnp.searchsorted(jnp.cumsum(ragged(own, 4, LEN, LEN // 2, 0)), jnp.arange(LEN), side="right"))(jax.random.split(seeds[1], SEQS)).reshape((SEQS, LEN)).astype(jnp.int32),
        "norm1_gain": jnp.clip(1.0 + 0.1 * jax.random.normal(seeds[2], (D,), jnp.float32), 0.5, 1.5).astype(jnp.bfloat16),
        "q_weight": bell_draw(seeds[3], (D, H * DK), D ** -0.5, 0.1875, ((0, 8), (1, 2))),
        "k_weight": bell_draw(seeds[4], (D, H * DK), D ** -0.5, 0.1875, ((0, 8), (1, 2))),
        "v_weight": bell_draw(seeds[5], (D, H * DV), D ** -0.5, 0.1875, ((0, 8), (1, 2))),
        "decay_weight": bell_draw(seeds[6], (D, H), D ** -0.5, 0.1875, ((0, 8), (1, 2))),
        "beta_weight": bell_draw(seeds[7], (D, H), D ** -0.5, 0.1875, ((0, 8), (1, 2))),
        "gate_weight": bell_draw(seeds[8], (D, H * DV), D ** -0.5, 0.1875, ((0, 8), (1, 2))),
        "conv_weight": bell_draw(seeds[9], (H * (2 * DK + DV), CONV), CONV ** -0.5, 3.0, ((0, 16),)),
        "decay_rate": jnp.clip(jnp.exp(math.log(0.05) - 4.6051702 * jax.random.uniform(seeds[10], (H,), jnp.float32) ** block_levels(seeds[10], (H,), ((0, 2),), -0.2, 0.2)), 0.0005, 0.05),
        "head_gain": jnp.clip(1.0 + 0.1 * jax.random.normal(seeds[11], (DV,), jnp.float32), 0.5, 1.5).astype(jnp.bfloat16),
        "out_weight": bell_draw(seeds[12], (D, H * DV), (H * DV // 4) ** -0.5, 0.25, ((0, 8), (1, 2))),
        "norm2_gain": jnp.clip(1.0 + 0.1 * jax.random.normal(seeds[13], (D,), jnp.float32), 0.5, 1.5).astype(jnp.bfloat16),
        "ffn_gate": bell_draw(seeds[14], (D, FF), D ** -0.5, 0.1875, ((0, 8), (1, 2))),
        "ffn_up": bell_draw(seeds[15], (D, FF), D ** -0.5, 0.1875, ((0, 8), (1, 2))),
        "ffn_down": bell_draw(seeds[16], (D, FF), FF ** -0.5, 0.109375, ((0, 8), (1, 2))),
        "cotangent": bell_draw(seeds[17], (SEQS, LEN, D), 1.0, 6.0, ((0, 8), (1, 2))),
    }


EPSILON = 1e-06
HIGHEST = lax.Precision.HIGHEST

def rms_scale(values, gain_vec):
    return values * lax.rsqrt(lax.optimization_barrier(jnp.mean(values * values, axis=-1, keepdims=True)) + EPSILON) * gain_vec

def unit_length(values):
    return values * lax.rsqrt(lax.optimization_barrier(jnp.sum(values * values, axis=-1, keepdims=True)) + EPSILON)

def swiglu(gate_in, up_in):
    return jax.nn.silu(gate_in) * up_in

def assemble(query_pre, key_pre, value_pre, head_count):
    length = query_pre.shape[0]
    joined = jnp.concatenate([query_pre.reshape(length, head_count, -1), key_pre.reshape(length, head_count, -1), value_pre.reshape(length, head_count, -1)], axis=2)
    return joined.reshape(length, -1)

def conv_front(mixed_pre, decay_pre, beta_pre, edge_pre, conv_taps, rate_vec, seg_value, edge_seg):
    taps_count = conv_taps.shape[1]
    length = mixed_pre.shape[0]
    head_count = decay_pre.shape[1]
    extended = jnp.concatenate([edge_pre, mixed_pre], axis=0)
    seg_ext = jnp.concatenate([edge_seg, seg_value], axis=0)
    mixed_sum = jnp.zeros_like(mixed_pre)
    for shift_back in range(taps_count):
        offset = taps_count - 1 - shift_back
        window = extended[offset:offset + length]
        same_doc = (seg_ext[offset:offset + length] == seg_value).astype(jnp.float32)
        mixed_sum = mixed_sum + conv_taps[:, shift_back] * window * same_doc[:, None]
    activated = jax.nn.silu(mixed_sum).reshape(length, head_count, -1)
    query_vec = unit_length(activated[:, :, :DK]) * DK ** (-0.5)
    key_vec = unit_length(activated[:, :, DK:2 * DK])
    value_vec = activated[:, :, 2 * DK:]
    beta_gate = jax.nn.sigmoid(beta_pre)
    log_decay = -rate_vec * jax.nn.softplus(decay_pre)
    return (query_vec, key_vec, value_vec, beta_gate, log_decay)

def split_blocks(array):
    blocks = array.shape[0] // GROUP
    shaped = array.reshape((blocks, GROUP) + array.shape[1:])
    return jnp.moveaxis(shaped, 2, 0)

def group_prep(query_vec, key_vec, value_vec, beta_gate, log_decay, seg_value, seg_before):
    query_blk = split_blocks(query_vec)
    key_blk = split_blocks(key_vec)
    value_blk = split_blocks(value_vec)
    beta_blk = split_blocks(beta_gate)
    decay_cum = jnp.cumsum(split_blocks(log_decay), axis=-1)
    seg_blk = seg_value.reshape(-1, GROUP)
    same_doc = seg_blk[:, :, None] == seg_blk[:, None, :]
    row_ids = lax.broadcasted_iota(jnp.int32, (GROUP, GROUP), 0)
    col_ids = lax.broadcasted_iota(jnp.int32, (GROUP, GROUP), 1)
    lower_mask = (row_ids >= col_ids) & same_doc
    strict = (row_ids > col_ids) & same_doc
    log_gap = decay_cum[..., :, None] - decay_cum[..., None, :]
    decay_pair = jnp.where(lower_mask, jnp.exp(jnp.where(lower_mask, log_gap, 0.0)), 0.0)
    decay_strict = jnp.where(strict, decay_pair, 0.0)
    from_start = jnp.where(seg_blk == seg_before[:, None], jnp.exp(decay_cum), 0.0)
    last_cum = decay_cum[..., -1:]
    to_end = jnp.where(seg_blk == seg_blk[:, -1:], jnp.exp(last_cum - decay_cum), 0.0)
    keep_whole = jnp.where(seg_blk[:, -1] == seg_before, jnp.exp(last_cum[..., 0]), 0.0)
    key_gram = jnp.einsum('hncd,hnjd->hncj', key_blk, key_blk, precision=HIGHEST)
    system = jnp.eye(GROUP, dtype=jnp.float32) + key_gram * decay_strict * beta_blk[..., :, None]
    wide_keys = lax.linalg.triangular_solve(system, (beta_blk * from_start)[..., None] * key_blk, left_side=True, lower=True, unit_diagonal=True)
    new_values = lax.linalg.triangular_solve(system, beta_blk[..., None] * value_blk, left_side=True, lower=True, unit_diagonal=True)
    scores = jnp.einsum('hncd,hnjd->hncj', query_blk, key_blk, precision=HIGHEST) * decay_pair
    query_dec = query_blk * from_start[..., None]
    key_dec = key_blk * to_end[..., None]
    return (wide_keys, new_values, scores, query_dec, key_dec, keep_whole)

def group_run(prepared, state_start):
    items = tuple((jnp.moveaxis(array, 1, 0) for array in prepared))

    def advance(state_now, block_items):
        wide_keys, new_values, scores, query_dec, key_dec, keep_whole = block_items
        fresh = new_values - jnp.einsum('hcd,hde->hce', wide_keys, state_now, precision=HIGHEST)
        result = jnp.einsum('hcd,hde->hce', query_dec, state_now, precision=HIGHEST) + jnp.einsum('hcj,hje->hce', scores, fresh, precision=HIGHEST)
        state_next = keep_whole[:, None, None] * state_now + jnp.einsum('hcd,hce->hde', key_dec, fresh, precision=HIGHEST)
        return (state_next, result)
    state_end, results = lax.scan(advance, state_start, items)
    blocks, head_count, width_c, width_v = results.shape
    return (jnp.transpose(results, (0, 2, 1, 3)).reshape(blocks * width_c, head_count, width_v), state_end)

def mixer_core(mixed_pre, decay_pre, beta_pre, edge_pre, conv_taps, rate_vec, state_start, seg_value, edge_seg):
    query_vec, key_vec, value_vec, beta_gate, log_decay = conv_front(mixed_pre, decay_pre, beta_pre, edge_pre, conv_taps, rate_vec, seg_value, edge_seg)
    seg_before = jnp.concatenate([edge_seg[-1:], seg_value[GROUP - 1::GROUP][:-1]])
    prepared = group_prep(query_vec, key_vec, value_vec, beta_gate, log_decay, seg_value, seg_before)
    return group_run(prepared, state_start)

def head_gate(outputs, gate_pre, gain_vec):
    normed = rms_scale(outputs, gain_vec)
    return (normed * jax.nn.silu(gate_pre.reshape(outputs.shape))).reshape(outputs.shape[0], -1)

def one_sequence(weights, row_input, row_seg, row_cot):
    gain_one, q_mat, k_mat, v_mat, decay_mat, beta_mat, gate_mat, conv_taps, rate_vec, gain_head, out_mat, gain_two, gate_ffn_mat, up_ffn_mat, down_ffn_mat = weights
    length = row_input.shape[0]
    head_count = decay_mat.shape[1]
    taps_count = conv_taps.shape[1]
    seg_value = row_seg.astype(jnp.float32)
    input_wide = row_input.astype(jnp.float32)
    norm_one, norm_one_back = jax.vjp(rms_scale, input_wide, gain_one.astype(jnp.float32))
    normed_one = norm_one.astype(jnp.bfloat16)
    matrices = (q_mat, k_mat, v_mat, decay_mat, beta_mat, gate_mat)
    projected = [jnp.dot(normed_one.astype(jnp.float32), matrix.astype(jnp.float32), preferred_element_type=jnp.float32) for matrix in matrices]
    query_pre, key_pre, value_pre, decay_pre, beta_pre, gate_pre = projected
    mixed_pre = assemble(query_pre, key_pre, value_pre, head_count)
    edge_pre = jnp.zeros((taps_count - 1, mixed_pre.shape[1]), jnp.float32)
    edge_seg = jnp.full((taps_count - 1,), -1.0, jnp.float32)
    state_zero = jnp.zeros((head_count, DK, DV), jnp.float32)

    def core_local(mixed_in, decay_in, beta_in, edge_in, taps_in, rate_in, state_in):
        return mixer_core(mixed_in, decay_in, beta_in, edge_in, taps_in, rate_in, state_in, seg_value, edge_seg)
    (outputs, final_state), core_back = jax.vjp(core_local, mixed_pre, decay_pre, beta_pre, edge_pre, conv_taps.astype(jnp.float32), rate_vec, state_zero)
    gated, gate_back = jax.vjp(head_gate, outputs, gate_pre, gain_head.astype(jnp.float32))
    gated_half = gated.astype(jnp.bfloat16)
    hidden = input_wide + jnp.dot(gated_half.astype(jnp.float32), out_mat.T.astype(jnp.float32), preferred_element_type=jnp.float32)
    norm_two, norm_two_back = jax.vjp(rms_scale, hidden, gain_two.astype(jnp.float32))
    normed_two = norm_two.astype(jnp.bfloat16)
    gate_ffn = jnp.dot(normed_two.astype(jnp.float32), gate_ffn_mat.astype(jnp.float32), preferred_element_type=jnp.float32)
    up_ffn = jnp.dot(normed_two.astype(jnp.float32), up_ffn_mat.astype(jnp.float32), preferred_element_type=jnp.float32)
    product, swiglu_back = jax.vjp(swiglu, gate_ffn, up_ffn)
    hidden_units = product.astype(jnp.bfloat16)
    block_out = (hidden + jnp.dot(hidden_units.astype(jnp.float32), down_ffn_mat.T.astype(jnp.float32), preferred_element_type=jnp.float32)).astype(jnp.bfloat16)
    d_units = jnp.dot(row_cot.astype(jnp.float32), down_ffn_mat.astype(jnp.float32), preferred_element_type=jnp.float32)
    g_down = jnp.dot(row_cot.T.astype(jnp.float32), hidden_units.astype(jnp.float32), preferred_element_type=jnp.float32)
    d_gate_ffn, d_up_ffn = swiglu_back(d_units)
    d_gate_half = d_gate_ffn.astype(jnp.bfloat16)
    d_up_half = d_up_ffn.astype(jnp.bfloat16)
    d_normed_two = jnp.dot(d_gate_half.astype(jnp.float32), gate_ffn_mat.T.astype(jnp.float32), preferred_element_type=jnp.float32) + jnp.dot(d_up_half.astype(jnp.float32), up_ffn_mat.T.astype(jnp.float32), preferred_element_type=jnp.float32)
    g_gate_ffn = jnp.dot(normed_two.T.astype(jnp.float32), d_gate_half.astype(jnp.float32), preferred_element_type=jnp.float32)
    g_up_ffn = jnp.dot(normed_two.T.astype(jnp.float32), d_up_half.astype(jnp.float32), preferred_element_type=jnp.float32)
    d_hidden_two, g_gain_two = norm_two_back(d_normed_two)
    d_hidden = row_cot.astype(jnp.float32) + d_hidden_two
    d_hidden_half = d_hidden.astype(jnp.bfloat16)
    d_gated = jnp.dot(d_hidden_half.astype(jnp.float32), out_mat.astype(jnp.float32), preferred_element_type=jnp.float32)
    g_out = jnp.dot(d_hidden_half.T.astype(jnp.float32), gated_half.astype(jnp.float32), preferred_element_type=jnp.float32)
    d_outputs, d_gate_pre, g_head = gate_back(d_gated)
    core_grads = core_back((d_outputs, jnp.zeros_like(final_state)))
    d_split = core_grads[0].reshape(length, head_count, -1)
    d_query = d_split[:, :, :DK].reshape(length, -1)
    d_key = d_split[:, :, DK:2 * DK].reshape(length, -1)
    d_value = d_split[:, :, 2 * DK:].reshape(length, -1)
    halves = [item.astype(jnp.bfloat16) for item in (d_query, d_key, d_value, core_grads[1], core_grads[2], d_gate_pre)]
    d_normed_one = jnp.zeros_like(input_wide)
    for half_item, matrix in zip(halves, matrices):
        d_normed_one = d_normed_one + jnp.dot(half_item.astype(jnp.float32), matrix.T.astype(jnp.float32), preferred_element_type=jnp.float32)
    weight_grads = [jnp.dot(normed_one.T.astype(jnp.float32), half_item.astype(jnp.float32), preferred_element_type=jnp.float32) for half_item in halves]
    d_input_one, g_gain_one = norm_one_back(d_normed_one)
    input_grad = d_hidden + d_input_one
    grads = (g_gain_one, weight_grads[0], weight_grads[1], weight_grads[2], weight_grads[3], weight_grads[4], weight_grads[5], core_grads[4], core_grads[5], g_head, g_out, g_gain_two, g_gate_ffn, g_up_ffn, g_down)
    return (block_out, input_grad, grads)

def reference(block_input, segments, norm1_gain, q_weight, k_weight, v_weight, decay_weight, beta_weight, gate_weight, conv_weight, decay_rate, head_gain, out_weight, norm2_gain, ffn_gate, ffn_up, ffn_down, cotangent):
    weights = (norm1_gain, q_weight, k_weight, v_weight, decay_weight, beta_weight, gate_weight, conv_weight, decay_rate, head_gain, out_weight, norm2_gain, ffn_gate, ffn_up, ffn_down)
    zero_grads = tuple((jnp.zeros(weight_item.shape, jnp.float32) for weight_item in weights))

    def per_sequence(totals, row_items):
        row_input, row_seg, row_cot = row_items
        block_out, input_grad, grads = one_sequence(weights, row_input, row_seg, row_cot)
        totals = tuple((total + grad_item for total, grad_item in zip(totals, grads)))
        return (totals, (block_out, input_grad))
    totals, stacked = lax.scan(per_sequence, zero_grads, (block_input, segments, cotangent))
    return (stacked[0], stacked[1], totals[0], totals[1], totals[2], totals[3], totals[4], totals[5], totals[6], totals[7], totals[8], totals[9], totals[10], totals[11], totals[12], totals[13], totals[14])
```

```python
import jax
import jax.numpy as jnp
from jax import lax
from jax.sharding import PartitionSpec as P

DK = 128
DV = 256
LANES = 128


EPSILON = 1e-06
HIGH = lax.Precision.HIGH


def shifted(block, axis, distance):
    devices = range(lax.axis_size(axis))
    route = [(i - distance, i) for i in devices if i - distance in devices]
    return lax.ppermute(block, axis, route)


def pair_sum(block, axis):
    sent = block.astype(jnp.bfloat16)
    if lax.axis_size(axis) != 2:
        return lax.psum(sent, axis).astype(jnp.float32)
    other = lax.ppermute(sent, axis, [(0, 1), (1, 0)])
    return sent.astype(jnp.float32) + other.astype(jnp.float32)


def rms_scale(values, gain_vec):
    return (
        values * lax.rsqrt(jnp.mean(values * values, axis=-1, keepdims=True) + EPSILON) * gain_vec
    )


def unit_length(values):
    return values * lax.rsqrt(jnp.sum(values * values, axis=-1, keepdims=True) + EPSILON)


def swiglu(gate_in, up_in):
    return jax.nn.silu(gate_in) * up_in


def dot32(left, right):
    return jnp.dot(left, right, preferred_element_type=jnp.float32)


def ein(spec, left, right):
    return jnp.einsum(spec, left, right, precision=HIGH)


def unit_inverse(strict_part):
    size = strict_part.shape[-1]
    rows = lax.broadcasted_iota(jnp.int32, (size, size), 0)
    cols = lax.broadcasted_iota(jnp.int32, (size, size), 1)
    eye = (rows == cols).astype(jnp.float32)
    inverse = eye - jnp.where(rows // 2 == cols // 2, strict_part, 0.0)
    width = 2
    while width < size:
        joins = (rows // (2 * width) == cols // (2 * width)) & (rows // width != cols // width)
        middle = jnp.where(joins, strict_part, 0.0)
        inverse = inverse - ein("hij,hjk->hik", ein("hij,hjk->hik", inverse, middle), inverse)
        width *= 2
    return inverse


@jax.custom_vjp
def unit_solve(strict_part, right):
    return ein("hij,hjd->hid", unit_inverse(strict_part), right)


def unit_solve_fwd(strict_part, right):
    inverse = unit_inverse(strict_part)
    solved = ein("hij,hjd->hid", inverse, right)
    return solved, (inverse, solved)


def unit_solve_bwd(kept, d_solved):
    inverse, solved = kept
    d_right = ein("hji,hjd->hid", inverse, d_solved)
    return -ein("hid,hjd->hij", d_right, solved), d_right


unit_solve.defvjp(unit_solve_fwd, unit_solve_bwd)


def by_head(flat, head_count):
    return jnp.moveaxis(flat.reshape(flat.shape[0], head_count, -1), 1, 0)


def prepare(mixed_pre, decay_pre, beta_pre, edge_pre, taps, rate_vec, seg_value, edge_seg):
    taps_count = taps.shape[0]
    length = mixed_pre.shape[0]
    head_count = decay_pre.shape[1]
    extended = jnp.concatenate([edge_pre, mixed_pre], axis=0)
    seg_ext = jnp.concatenate([edge_seg, seg_value], axis=0)
    mixed_sum = jnp.zeros_like(mixed_pre)
    for shift_back in range(taps_count):
        offset = taps_count - 1 - shift_back
        window = extended[offset : offset + length]
        same_doc = (seg_ext[offset : offset + length] == seg_value).astype(jnp.float32)
        mixed_sum = mixed_sum + taps[shift_back] * window * same_doc[:, None]
    activated = jax.nn.silu(mixed_sum)
    width = head_count * DK
    query = unit_length(by_head(activated[:, :width], head_count)) * DK ** (-0.5)
    key = unit_length(by_head(activated[:, width : 2 * width], head_count))
    value = by_head(activated[:, 2 * width :], head_count)
    beta = jax.nn.sigmoid(beta_pre).T
    log_decay = (-rate_vec * jax.nn.softplus(decay_pre)).T
    decay_cum = jnp.cumsum(log_decay, axis=-1)
    same_doc = seg_value[:, None] == seg_value[None, :]
    rows = lax.broadcasted_iota(jnp.int32, (length, length), 0)
    cols = lax.broadcasted_iota(jnp.int32, (length, length), 1)
    lower_mask = (rows >= cols) & same_doc
    log_gap = decay_cum[:, :, None] - decay_cum[:, None, :]
    decay_pair = jnp.where(lower_mask, jnp.exp(jnp.where(lower_mask, log_gap, 0.0)), 0.0)
    decay_strict = jnp.where(rows > cols, decay_pair, 0.0)
    from_start = jnp.where(seg_value == edge_seg[-1], jnp.exp(decay_cum), 0.0)
    last_cum = decay_cum[:, -1:]
    to_end = jnp.where(seg_value == seg_value[-1], jnp.exp(last_cum - decay_cum), 0.0)
    keep_whole = jnp.where(seg_value[-1] == edge_seg[-1], jnp.exp(last_cum[:, 0]), 0.0)
    key_gram = ein("hid,hjd->hij", key, key)
    strict_part = key_gram * decay_strict * beta[:, :, None]
    right = beta[:, :, None] * jnp.concatenate([from_start[:, :, None] * key, value], axis=2)
    solved = unit_solve(strict_part, right)
    scores = ein("hid,hjd->hij", query, key) * decay_pair
    query_dec = query * from_start[:, :, None]
    key_dec = key * to_end[:, :, None]
    return solved, scores, query_dec, key_dec, keep_whole


def head_gate(outputs, gate_pre, gain_vec):
    rows = jnp.moveaxis(outputs, 0, 1)
    normed = rms_scale(rows, gain_vec)
    return (normed * jax.nn.silu(gate_pre.reshape(rows.shape))).reshape(rows.shape[0], -1)


def as_column(vector, rows):
    return jnp.pad(vector, (0, rows - vector.shape[0]))[:, None]


def gather(shard):
    return lax.all_gather(shard, "fsdp", axis=0, tiled=True)


def scatter(whole):
    return lax.psum_scatter(
        whole.astype(jnp.bfloat16), "fsdp", scatter_dimension=0, tiled=True
    )


def per_device(
    block_input,
    segments,
    norm1_gain,
    q_weight,
    k_weight,
    v_weight,
    decay_weight,
    beta_weight,
    gate_weight,
    conv_weight,
    decay_rate,
    head_gain,
    out_weight,
    norm2_gain,
    ffn_gate,
    ffn_up,
    ffn_down,
    cotangent,
):
    fsdp = lax.axis_size("fsdp")
    ctx = lax.axis_size("ctx")
    rows = q_weight.shape[0]
    head_count = decay_weight.shape[1]
    taps_count = conv_weight.shape[1]
    q_cols = q_weight.shape[1]
    qk_cols = q_cols + k_weight.shape[1]
    pre_cols = qk_cols + v_weight.shape[1]
    gate_cols = gate_weight.shape[1]
    ffn_cols = ffn_gate.shape[1]
    small = [
        decay_weight,
        beta_weight,
        norm1_gain[:, None],
        norm2_gain[:, None],
        as_column(head_gain, rows),
        conv_weight.reshape(rows, -1),
    ]
    small_used = sum(piece.shape[1] for piece in small)
    small_cols = -(-small_used // LANES) * LANES
    small.append(jnp.zeros((rows, small_cols - small_used), jnp.bfloat16))
    first_shard = jnp.concatenate([q_weight, k_weight, v_weight] + small, axis=1)
    first_mat = gather(first_shard)
    second_shard, _ = lax.optimization_barrier((jnp.concatenate([gate_weight, out_weight], axis=1), first_shard))
    second_mat = gather(second_shard)
    third_mat = gather(jnp.concatenate([ffn_gate, ffn_up], axis=1))
    down_mat = gather(ffn_down)
    gate_mat, out_mat = second_mat[:, :gate_cols], second_mat[:, gate_cols:]
    small_mat = first_mat[:, pre_cols:]
    heads2 = 2 * head_count
    gain_one = small_mat[:, heads2].astype(jnp.float32)
    gain_two = small_mat[:, heads2 + 1].astype(jnp.float32)
    head_len = head_gain.shape[0]
    gain_head = (
        small_mat[:, heads2 + 2].reshape(fsdp, rows)[:, :head_len].reshape(-1).astype(jnp.float32)
    )
    conv_cols = conv_weight.shape[0] * taps_count // rows
    conv_taps = small_mat[:, heads2 + 3 : heads2 + 3 + conv_cols].reshape(-1, taps_count)

    row_input = block_input[0]
    seg_value = segments[0].astype(jnp.float32)
    row_cot = cotangent[0]
    length = row_input.shape[0]
    tail_start = length - taps_count + 1
    input_wide = row_input.astype(jnp.float32)
    norm_one, norm_one_back = jax.vjp(rms_scale, input_wide, gain_one)
    normed_one = norm_one.astype(jnp.bfloat16)
    projected = dot32(normed_one, first_mat)
    mixed_pre = projected[:, :pre_cols]
    decay_pre = projected[:, pre_cols : pre_cols + head_count]
    beta_pre = projected[:, pre_cols + head_count : pre_cols + heads2]
    edge_pre, edge_seg = shifted((mixed_pre[tail_start:], seg_value[tail_start:]), "ctx", 1)

    def to_taps(by_channel):
        grouped = by_channel.T.reshape(taps_count, head_count, -1)
        return jnp.concatenate(
            [
                grouped[:, :, :DK].reshape(taps_count, -1),
                grouped[:, :, DK : 2 * DK].reshape(taps_count, -1),
                grouped[:, :, 2 * DK :].reshape(taps_count, -1),
            ],
            axis=1,
        )

    def prepare_local(mixed_in, decay_in, beta_in, edge_in, taps_in, rate_in):
        return prepare(
            mixed_in, decay_in, beta_in, edge_in, to_taps(taps_in), rate_in, seg_value, edge_seg
        )

    (solved, scores, query_dec, key_dec, keep_whole), prepare_back = jax.vjp(
        prepare_local,
        mixed_pre,
        decay_pre,
        beta_pre,
        edge_pre,
        conv_taps.astype(jnp.float32),
        decay_rate,
    )
    wide_keys, new_values = solved[:, :, :DK], solved[:, :, DK:]
    state_zero = jnp.zeros((head_count, DK, DV), jnp.float32)
    carried = ein("hcd,hce->hde", key_dec, new_values)
    if ctx > 2:
        moved = keep_whole[:, None, None] * jnp.eye(DK, dtype=jnp.float32) - ein(
            "hcd,hce->hde", key_dec, wide_keys
        )

    def pass_on(total, distance):
        return shifted(total.astype(jnp.bfloat16), "ctx", distance).astype(jnp.float32)

    state_start = pass_on(carried, 1) if ctx > 1 else state_zero
    for _ in range(ctx - 2):
        state_start = pass_on(ein("hde,hef->hdf", moved, state_start) + carried, 1)
    gate_pre = dot32(normed_one, gate_mat)
    fresh = new_values - ein("hcd,hde->hce", wide_keys, state_start)
    outputs = ein("hcd,hde->hce", query_dec, state_start) + ein("hcj,hje->hce", scores, fresh)
    gated, gate_back = jax.vjp(head_gate, outputs, gate_pre, gain_head)
    gated_half = gated.astype(jnp.bfloat16)
    mixer_out = pair_sum(dot32(gated_half, out_mat.T), "tp")
    hidden = input_wide + mixer_out
    norm_two, norm_two_back = jax.vjp(rms_scale, hidden, gain_two)
    normed_two = norm_two.astype(jnp.bfloat16)
    both_ffn = dot32(normed_two, third_mat)
    product, swiglu_back = jax.vjp(swiglu, both_ffn[:, :ffn_cols], both_ffn[:, ffn_cols:])
    hidden_units = product.astype(jnp.bfloat16)
    d_units = dot32(row_cot, down_mat)
    d_gate_ffn, d_up_ffn = swiglu_back(d_units)
    d_both_half = jnp.concatenate(
        [d_gate_ffn.astype(jnp.bfloat16), d_up_ffn.astype(jnp.bfloat16)], axis=1
    )
    d_normed_two = pair_sum(dot32(d_both_half, third_mat.T), "tp")
    ffn_out = pair_sum(dot32(hidden_units, down_mat.T), "tp")
    block_out = (hidden + ffn_out).astype(jnp.bfloat16)
    g_down = dot32(row_cot.T, hidden_units)
    g_both = dot32(normed_two.T, d_both_half)
    ffn_shards = scatter(jnp.concatenate([g_down.astype(jnp.bfloat16), g_both.astype(jnp.bfloat16)], axis=1))
    d_hidden_two, g_gain_two = norm_two_back(d_normed_two)
    d_hidden = row_cot.astype(jnp.float32) + d_hidden_two
    d_hidden_half = d_hidden.astype(jnp.bfloat16)
    d_gated = dot32(d_hidden_half, out_mat)
    d_outputs, d_gate_pre, g_head_part = gate_back(d_gated)
    d_gate_half = d_gate_pre.astype(jnp.bfloat16)
    g_out = dot32(d_hidden_half.T, gated_half)
    g_gate = dot32(normed_one.T, d_gate_half)
    second_shards = scatter(jnp.concatenate([g_gate.astype(jnp.bfloat16), g_out.astype(jnp.bfloat16)], axis=1))

    d_fresh_local = ein("hcj,hce->hje", scores, d_outputs)
    local_start = ein("hcd,hce->hde", query_dec, d_outputs) - ein(
        "hcd,hce->hde", wide_keys, d_fresh_local
    )
    state_grad = pass_on(local_start, -1) if ctx > 1 else state_zero
    for _ in range(ctx - 2):
        state_grad = pass_on(ein("hed,hef->hdf", moved, state_grad) + local_start, -1)
    d_fresh = d_fresh_local + ein("hcd,hde->hce", key_dec, state_grad)
    d_solved = jnp.concatenate([-ein("hce,hde->hcd", d_fresh, state_start), d_fresh], axis=2)
    d_scores = ein("hce,hje->hcj", d_outputs, fresh)
    d_query_dec = ein("hce,hde->hcd", d_outputs, state_start)
    d_key_dec = ein("hce,hde->hcd", fresh, state_grad)
    d_keep = jnp.sum(state_start * state_grad, axis=(1, 2))
    d_mixed, d_decay, d_beta, d_edge, g_conv, g_rate = prepare_back(
        (d_solved, d_scores, d_query_dec, d_key_dec, d_keep)
    )
    edge_grad = shifted(d_edge, "ctx", -1)
    d_mixed = d_mixed + jnp.pad(edge_grad, ((tail_start, 0), (0, 0)))
    half_first = jnp.concatenate(
        [
            d_mixed.astype(jnp.bfloat16),
            d_decay.astype(jnp.bfloat16),
            d_beta.astype(jnp.bfloat16),
            jnp.zeros((length, small_cols - heads2), jnp.bfloat16),
        ],
        axis=1,
    )
    d_first_part = dot32(half_first, first_mat.T) + dot32(d_gate_half, gate_mat.T)
    d_normed_one = pair_sum(d_first_part, "tp")
    g_first = dot32(normed_one.T, half_first[:, : pre_cols + heads2])
    d_input_one, _ = norm_one_back(d_normed_one)
    _, g_gain_one = norm_one_back(d_first_part)
    input_grad = d_hidden + d_input_one
    head_part = jnp.pad(g_head_part.reshape(fsdp, head_len), ((0, 0), (0, rows - head_len)))
    extra = jnp.concatenate(
        [
            g_gain_one[:, None],
            g_gain_two[:, None],
            head_part.reshape(-1, 1),
            g_conv.reshape(fsdp * rows, -1),
            jnp.broadcast_to(g_rate[None], (fsdp * rows, head_count)),
        ],
        axis=1,
    )
    pad_cols = small_cols - heads2 - extra.shape[1]
    first_shards = scatter(
        jnp.concatenate(
            [
                g_first.astype(jnp.bfloat16),
                jnp.pad(extra, ((0, 0), (0, pad_cols))).astype(jnp.bfloat16),
            ],
            axis=1,
        )
    )
    ffn_sum = pair_sum(ffn_shards, "ctx")
    second_sum = pair_sum(second_shards, "ctx")
    first_sum = pair_sum(first_shards, "ctx")
    small_sum = first_sum[:, pre_cols:]
    shared = pair_sum(small_sum[:, heads2 : heads2 + 3], "tp")
    conv_end = heads2 + 3 + conv_cols
    return (
        block_out[None],
        input_grad[None],
        shared[:, 0],
        first_sum[:, :q_cols],
        first_sum[:, q_cols:qk_cols],
        first_sum[:, qk_cols:pre_cols],
        small_sum[:, :head_count],
        small_sum[:, head_count:heads2],
        second_sum[:, :gate_cols],
        small_sum[:, heads2 + 3 : conv_end].reshape(conv_weight.shape),
        small_sum[0, conv_end : conv_end + head_count],
        shared[:head_len, 2],
        second_sum[:, gate_cols:],
        small_sum[:, heads2 + 1],
        ffn_sum[:, ffn_cols : 2 * ffn_cols],
        ffn_sum[:, 2 * ffn_cols :],
        ffn_sum[:, :ffn_cols],
    )


def solution(mesh):
    placed = (
        P("fsdp", "ctx", None),
        P("fsdp", "ctx"),
        P("fsdp"),
        P("fsdp", "tp"),
        P("fsdp", "tp"),
        P("fsdp", "tp"),
        P("fsdp", "tp"),
        P("fsdp", "tp"),
        P("fsdp", "tp"),
        P(("tp", "fsdp"), None),
        P("tp"),
        P("fsdp"),
        P("fsdp", "tp"),
        P("fsdp"),
        P("fsdp", "tp"),
        P("fsdp", "tp"),
        P("fsdp", "tp"),
        P("fsdp", "ctx", None),
    )
    return jax.shard_map(
        per_device,
        mesh=mesh,
        in_specs=placed,
        out_specs=(
            P("fsdp", "ctx", None),
            P("fsdp", "ctx", None),
            P("fsdp"),
            P("fsdp", "tp"),
            P("fsdp", "tp"),
            P("fsdp", "tp"),
            P("fsdp", "tp"),
            P("fsdp", "tp"),
            P("fsdp", "tp"),
            P(("tp", "fsdp"), None),
            P("tp"),
            P("fsdp"),
            P("fsdp", "tp"),
            P("fsdp"),
            P("fsdp", "tp"),
            P("fsdp", "tp"),
            P("fsdp", "tp"),
        ),
        check_vma=False,
    )
```

```python
import jax
import jax.numpy as jnp
from jax import lax
from jax.sharding import PartitionSpec as P


DK = 128
DV = 256
LANES = 128


EPSILON = 1e-06
HIGH = lax.Precision.HIGH


def shifted(block, axis, distance):
    devices = range(lax.axis_size(axis))
    route = [(i - distance, i) for i in devices if i - distance in devices]
    return lax.ppermute(block, axis, route)


def pair_sum(block, axis):
    sent = lax.optimization_barrier(block.astype(jnp.bfloat16))
    if lax.axis_size(axis) != 2:
        return lax.psum(sent, axis).astype(jnp.float32)
    other = lax.ppermute(sent, axis, [(0, 1), (1, 0)])
    return sent.astype(jnp.float32) + other.astype(jnp.float32)


def rms_scale(values, gain_vec):
    return (
        values * lax.rsqrt(jnp.mean(values * values, axis=-1, keepdims=True) + EPSILON) * gain_vec
    )


def unit_length(values):
    return values * lax.rsqrt(jnp.sum(values * values, axis=-1, keepdims=True) + EPSILON)


def swiglu(gate_in, up_in):
    return jax.nn.silu(gate_in) * up_in


def dot32(left, right):
    return jnp.dot(left, right, preferred_element_type=jnp.float32)


def ein(spec, left, right):
    return jnp.einsum(spec, left, right, precision=HIGH)


def unit_inverse(strict_part):
    size = strict_part.shape[-1]
    rows = lax.broadcasted_iota(jnp.int32, (size, size), 0)
    cols = lax.broadcasted_iota(jnp.int32, (size, size), 1)
    eye = (rows == cols).astype(jnp.float32)
    inverse = eye - jnp.where(rows // 2 == cols // 2, strict_part, 0.0)
    width = 2
    while width < size:
        joins = (rows // (2 * width) == cols // (2 * width)) & (rows // width != cols // width)
        middle = jnp.where(joins, strict_part, 0.0)
        inverse = inverse - ein("hij,hjk->hik", ein("hij,hjk->hik", inverse, middle), inverse)
        width *= 2
    return inverse


@jax.custom_vjp
def unit_solve(strict_part, right):
    return ein("hij,hjd->hid", unit_inverse(strict_part), right)


def unit_solve_fwd(strict_part, right):
    inverse = unit_inverse(strict_part)
    solved = ein("hij,hjd->hid", inverse, right)
    return solved, (inverse, solved)


def unit_solve_bwd(kept, d_solved):
    inverse, solved = kept
    d_right = ein("hji,hjd->hid", inverse, d_solved)
    return -ein("hid,hjd->hij", d_right, solved), d_right


unit_solve.defvjp(unit_solve_fwd, unit_solve_bwd)


def by_head(flat, head_count):
    return jnp.moveaxis(flat.reshape(flat.shape[0], head_count, -1), 1, 0)


def prepare(mixed_pre, decay_pre, beta_pre, edge_pre, taps, rate_vec, seg_value, edge_seg):
    taps_count = taps.shape[0]
    length = mixed_pre.shape[0]
    head_count = decay_pre.shape[1]
    extended = jnp.concatenate([edge_pre, mixed_pre], axis=0)
    seg_ext = jnp.concatenate([edge_seg, seg_value], axis=0)
    mixed_sum = jnp.zeros_like(mixed_pre)
    for shift_back in range(taps_count):
        offset = taps_count - 1 - shift_back
        window = extended[offset : offset + length]
        same_doc = (seg_ext[offset : offset + length] == seg_value).astype(jnp.float32)
        mixed_sum = mixed_sum + taps[shift_back] * window * same_doc[:, None]
    activated = jax.nn.silu(mixed_sum)
    width = head_count * DK
    query = unit_length(by_head(activated[:, :width], head_count)) * DK ** (-0.5)
    key = unit_length(by_head(activated[:, width : 2 * width], head_count))
    value = by_head(activated[:, 2 * width :], head_count)
    beta = jax.nn.sigmoid(beta_pre).T
    log_decay = (-rate_vec * jax.nn.softplus(decay_pre)).T
    decay_cum = running_sum(log_decay)
    same_doc = seg_value[:, None] == seg_value[None, :]
    rows = lax.broadcasted_iota(jnp.int32, (length, length), 0)
    cols = lax.broadcasted_iota(jnp.int32, (length, length), 1)
    lower_mask = (rows >= cols) & same_doc
    log_gap = decay_cum[:, :, None] - decay_cum[:, None, :]
    decay_pair = jnp.where(lower_mask, jnp.exp(jnp.where(lower_mask, log_gap, 0.0)), 0.0)
    decay_strict = jnp.where(rows > cols, decay_pair, 0.0)
    from_start = jnp.where(seg_value == edge_seg[-1], jnp.exp(decay_cum), 0.0)
    last_cum = decay_cum[:, -1:]
    to_end = jnp.where(seg_value == seg_value[-1], jnp.exp(last_cum - decay_cum), 0.0)
    keep_whole = jnp.where(seg_value[-1] == edge_seg[-1], jnp.exp(last_cum[:, 0]), 0.0)
    key_gram = ein("hid,hjd->hij", key, key)
    strict_part = key_gram * decay_strict * beta[:, :, None]
    right = beta[:, :, None] * jnp.concatenate([from_start[:, :, None] * key, value], axis=2)
    solved = unit_solve(strict_part, right)
    scores = ein("hid,hjd->hij", query, key) * decay_pair
    query_dec = query * from_start[:, :, None]
    key_dec = key * to_end[:, :, None]
    return solved, scores, query_dec, key_dec, keep_whole


def head_gate(outputs, gate_pre, gain_vec):
    rows = jnp.moveaxis(outputs, 0, 1)
    normed = rms_scale(rows, gain_vec)
    return (normed * jax.nn.silu(gate_pre.reshape(rows.shape))).reshape(rows.shape[0], -1)


def as_column(vector, rows):
    return jnp.pad(vector, (0, rows - vector.shape[0]))[:, None]


def gather(shard):
    return lax.all_gather(shard, "fsdp", axis=0, tiled=True)


def scatter(whole):
    return lax.psum_scatter(
        whole.astype(jnp.bfloat16), "fsdp", scatter_dimension=0, tiled=True
    )


def dot16(left, right):
    return jnp.dot(left, right, preferred_element_type=jnp.bfloat16)


def running_sum(values):
    size = values.shape[-1]
    rows = lax.broadcasted_iota(jnp.int32, (size, size), 0)
    cols = lax.broadcasted_iota(jnp.int32, (size, size), 1)
    upper = (rows <= cols).astype(jnp.float32)
    return jnp.dot(values, upper, precision=lax.Precision.HIGHEST)


def per_device(
    block_input,
    segments,
    norm1_gain,
    q_weight,
    k_weight,
    v_weight,
    decay_weight,
    beta_weight,
    gate_weight,
    conv_weight,
    decay_rate,
    head_gain,
    out_weight,
    norm2_gain,
    ffn_gate,
    ffn_up,
    ffn_down,
    cotangent,
):
    fsdp = lax.axis_size("fsdp")
    ctx = lax.axis_size("ctx")
    rows = q_weight.shape[0]
    head_count = decay_weight.shape[1]
    taps_count = conv_weight.shape[1]
    q_cols = q_weight.shape[1]
    qk_cols = q_cols + k_weight.shape[1]
    pre_cols = qk_cols + v_weight.shape[1]
    ffn_cols = ffn_gate.shape[1]
    small = [
        decay_weight,
        beta_weight,
        norm1_gain[:, None],
        norm2_gain[:, None],
        as_column(head_gain, rows),
        conv_weight.reshape(rows, -1),
    ]
    small_used = sum(piece.shape[1] for piece in small)
    small_cols = -(-small_used // LANES) * LANES
    small.append(jnp.zeros((rows, small_cols - small_used), jnp.bfloat16))
    first_shard = jnp.concatenate([q_weight, k_weight, v_weight] + small, axis=1)
    first_mat = gather(first_shard)
    gate_mat = gather(gate_weight)
    out_mat = gather(out_weight)
    third_mat = gather(jnp.concatenate([ffn_gate, ffn_up], axis=1))
    down_mat = gather(ffn_down)
    small_mat = first_mat[:, pre_cols:]
    heads2 = 2 * head_count
    gain_one = small_mat[:, heads2].astype(jnp.float32)
    gain_two = small_mat[:, heads2 + 1].astype(jnp.float32)
    head_len = head_gain.shape[0]
    gain_head = (
        small_mat[:, heads2 + 2].reshape(fsdp, rows)[:, :head_len].reshape(-1).astype(jnp.float32)
    )
    conv_cols = conv_weight.shape[0] * taps_count // rows
    conv_taps = small_mat[:, heads2 + 3 : heads2 + 3 + conv_cols].reshape(-1, taps_count)

    row_input = block_input[0]
    seg_value = segments[0].astype(jnp.float32)
    row_cot = cotangent[0]
    length = row_input.shape[0]
    tail_start = length - taps_count + 1
    input_wide = row_input.astype(jnp.float32)
    norm_one, norm_one_back = jax.vjp(rms_scale, input_wide, gain_one)
    normed_one = norm_one.astype(jnp.bfloat16)
    projected = dot32(normed_one, first_mat)
    mixed_pre = projected[:, :pre_cols]
    decay_pre = projected[:, pre_cols : pre_cols + head_count]
    beta_pre = projected[:, pre_cols + head_count : pre_cols + heads2]
    edge_pre, edge_seg = shifted((mixed_pre[tail_start:], seg_value[tail_start:]), "ctx", 1)

    def to_taps(by_channel):
        grouped = by_channel.T.reshape(taps_count, head_count, -1)
        return jnp.concatenate(
            [
                grouped[:, :, :DK].reshape(taps_count, -1),
                grouped[:, :, DK : 2 * DK].reshape(taps_count, -1),
                grouped[:, :, 2 * DK :].reshape(taps_count, -1),
            ],
            axis=1,
        )

    def prepare_local(mixed_in, decay_in, beta_in, edge_in, taps_in, rate_in):
        return prepare(
            mixed_in, decay_in, beta_in, edge_in, to_taps(taps_in), rate_in, seg_value, edge_seg
        )

    (solved, scores, query_dec, key_dec, keep_whole), prepare_back = jax.vjp(
        prepare_local,
        mixed_pre,
        decay_pre,
        beta_pre,
        edge_pre,
        conv_taps.astype(jnp.float32),
        decay_rate,
    )
    wide_keys, new_values = solved[:, :, :DK], solved[:, :, DK:]
    state_zero = jnp.zeros((head_count, DK, DV), jnp.float32)
    carried = ein("hcd,hce->hde", key_dec, new_values)
    if ctx > 2:
        moved = keep_whole[:, None, None] * jnp.eye(DK, dtype=jnp.float32) - ein(
            "hcd,hce->hde", key_dec, wide_keys
        )

    def pass_on(total, distance):
        return shifted(total.astype(jnp.bfloat16), "ctx", distance).astype(jnp.float32)

    state_start = pass_on(carried, 1) if ctx > 1 else state_zero
    for _ in range(ctx - 2):
        state_start = pass_on(ein("hde,hef->hdf", moved, state_start) + carried, 1)
    gate_pre = dot32(normed_one, gate_mat)
    fresh = new_values - ein("hcd,hde->hce", wide_keys, state_start)
    outputs = ein("hcd,hde->hce", query_dec, state_start) + ein("hcj,hje->hce", scores, fresh)
    gated, gate_back = jax.vjp(head_gate, outputs, gate_pre, gain_head)
    gated_half = gated.astype(jnp.bfloat16)
    mixer_out = pair_sum(dot32(gated_half, out_mat.T), "tp")
    hidden = input_wide + mixer_out
    norm_two, norm_two_back = jax.vjp(rms_scale, hidden, gain_two)
    normed_two = norm_two.astype(jnp.bfloat16)
    both_ffn = dot32(normed_two, third_mat)
    product, swiglu_back = jax.vjp(swiglu, both_ffn[:, :ffn_cols], both_ffn[:, ffn_cols:])
    hidden_units = product.astype(jnp.bfloat16)
    d_units = dot32(row_cot, down_mat)
    d_gate_ffn, d_up_ffn = swiglu_back(d_units)
    d_both_half = jnp.concatenate(
        [d_gate_ffn.astype(jnp.bfloat16), d_up_ffn.astype(jnp.bfloat16)], axis=1
    )
    units_wide = jnp.pad(hidden_units, ((0, 0), (0, -ffn_cols % (2 * LANES))))
    g_down = dot16(row_cot.T, units_wide)
    down_shards = scatter(g_down)
    d_normed_part = dot32(d_both_half, third_mat.T).astype(jnp.bfloat16)
    g_both = dot16(normed_two.T, d_both_half)
    both_shards = scatter(g_both)
    d_normed_two = pair_sum(d_normed_part, "tp")
    d_normed_two, _, _ = lax.optimization_barrier((d_normed_two, g_both, g_down))
    ffn_out = pair_sum(dot32(hidden_units, down_mat.T), "tp")
    block_out = (hidden + ffn_out).astype(jnp.bfloat16)
    d_hidden_two, g_gain_two = norm_two_back(d_normed_two)
    d_hidden = row_cot.astype(jnp.float32) + d_hidden_two
    d_hidden_half = d_hidden.astype(jnp.bfloat16)
    d_gated = dot32(d_hidden_half, out_mat)
    d_outputs, d_gate_pre, g_head_part = gate_back(d_gated)
    d_gate_half = d_gate_pre.astype(jnp.bfloat16)
    g_out = dot16(d_hidden_half.T, gated_half)
    out_shards = scatter(g_out)
    g_gate = dot16(normed_one.T, d_gate_half)
    gate_shards = scatter(g_gate)
    d_outputs, _, _ = lax.optimization_barrier((d_outputs, g_out, g_gate))

    d_fresh_local = ein("hcj,hce->hje", scores, d_outputs)
    local_start = ein("hcd,hce->hde", query_dec, d_outputs) - ein(
        "hcd,hce->hde", wide_keys, d_fresh_local
    )
    state_grad = pass_on(local_start, -1) if ctx > 1 else state_zero
    for _ in range(ctx - 2):
        state_grad = pass_on(ein("hed,hef->hdf", moved, state_grad) + local_start, -1)
    d_fresh = d_fresh_local + ein("hcd,hde->hce", key_dec, state_grad)
    d_solved = jnp.concatenate([-ein("hce,hde->hcd", d_fresh, state_start), d_fresh], axis=2)
    d_scores = ein("hce,hje->hcj", d_outputs, fresh)
    d_query_dec = ein("hce,hde->hcd", d_outputs, state_start)
    d_key_dec = ein("hce,hde->hcd", fresh, state_grad)
    d_keep = jnp.sum(state_start * state_grad, axis=(1, 2))
    d_mixed, d_decay, d_beta, d_edge, g_conv, g_rate = prepare_back(
        (d_solved, d_scores, d_query_dec, d_key_dec, d_keep)
    )
    edge_grad = shifted(d_edge, "ctx", -1)
    rate_sum = lax.psum(g_rate, ("fsdp", "ctx"))
    d_mixed = d_mixed + jnp.pad(edge_grad, ((tail_start, 0), (0, 0)))
    half_first = jnp.concatenate(
        [
            d_mixed.astype(jnp.bfloat16),
            d_decay.astype(jnp.bfloat16),
            d_beta.astype(jnp.bfloat16),
            jnp.zeros((length, small_cols - heads2), jnp.bfloat16),
        ],
        axis=1,
    )
    d_first_part = dot32(half_first, first_mat.T) + dot32(d_gate_half, gate_mat.T)
    d_normed_one = pair_sum(d_first_part, "tp")
    d_input_one, _ = norm_one_back(d_normed_one)
    _, g_gain_one = norm_one_back(d_first_part)
    input_grad = d_hidden + d_input_one
    head_part = jnp.pad(g_head_part.reshape(fsdp, head_len), ((0, 0), (0, rows - head_len)))
    extra = jnp.concatenate(
        [
            g_gain_one[:, None],
            g_gain_two[:, None],
            head_part.reshape(-1, 1),
            g_conv.reshape(fsdp * rows, -1),
        ],
        axis=1,
    )
    wide_half = jnp.pad(half_first, ((0, 0), (0, -half_first.shape[1] % (2 * LANES))))
    g_first = dot16(normed_one.T, wide_half)
    g_first = lax.dynamic_update_slice(
        g_first, extra.astype(jnp.bfloat16), (0, pre_cols + heads2)
    )
    first_shards = scatter(g_first)
    down_sum = pair_sum(down_shards, "ctx")
    both_sum = pair_sum(both_shards, "ctx")
    out_sum = pair_sum(out_shards, "ctx")
    gate_sum = pair_sum(gate_shards, "ctx")
    first_sum = pair_sum(first_shards, "ctx")
    small_sum = first_sum[:, pre_cols:]
    shared = pair_sum(small_sum[:, heads2 : heads2 + 3], "tp")
    conv_end = heads2 + 3 + conv_cols
    return (
        block_out[None],
        input_grad[None],
        shared[:, 0],
        first_sum[:, :q_cols],
        first_sum[:, q_cols:qk_cols],
        first_sum[:, qk_cols:pre_cols],
        small_sum[:, :head_count],
        small_sum[:, head_count:heads2],
        gate_sum,
        small_sum[:, heads2 + 3 : conv_end].reshape(conv_weight.shape),
        rate_sum,
        shared[:head_len, 2],
        out_sum,
        small_sum[:, heads2 + 1],
        both_sum[:, :ffn_cols],
        both_sum[:, ffn_cols:],
        down_sum[:, :ffn_cols],
    )


def solution(mesh):
    placed = (
        P("fsdp", "ctx", None),
        P("fsdp", "ctx"),
        P("fsdp"),
        P("fsdp", "tp"),
        P("fsdp", "tp"),
        P("fsdp", "tp"),
        P("fsdp", "tp"),
        P("fsdp", "tp"),
        P("fsdp", "tp"),
        P(("tp", "fsdp"), None),
        P("tp"),
        P("fsdp"),
        P("fsdp", "tp"),
        P("fsdp"),
        P("fsdp", "tp"),
        P("fsdp", "tp"),
        P("fsdp", "tp"),
        P("fsdp", "ctx", None),
    )
    return jax.shard_map(
        per_device,
        mesh=mesh,
        in_specs=placed,
        out_specs=(
            P("fsdp", "ctx", None),
            P("fsdp", "ctx", None),
            P("fsdp"),
            P("fsdp", "tp"),
            P("fsdp", "tp"),
            P("fsdp", "tp"),
            P("fsdp", "tp"),
            P("fsdp", "tp"),
            P("fsdp", "tp"),
            P(("tp", "fsdp"), None),
            P("tp"),
            P("fsdp"),
            P("fsdp", "tp"),
            P("fsdp"),
            P("fsdp", "tp"),
            P("fsdp", "tp"),
            P("fsdp", "tp"),
        ),
        check_vma=False,
    )
```
